128 devices in a mesh: seq: 32 (over x, y, core), head: 4 (over z).
Axes of the slice: x: 4, y: 4, z: 4, core: 2. Of those that a mesh axis runs over, the one named last changes fastest.
Arguments:
- queries: bfloat16 [16384, 4096], P('seq', 'head'), may hold values from -7 to 7
- keys: bfloat16 [131072, 1024], P('seq', 'head'), may hold values from -4 to 4
- values: bfloat16 [131072, 1024], P('seq', 'head'), may hold values from -5 to 5
- out_grad: bfloat16 [16384, 4096], P('seq', 'head'), may hold values from -6 to 6
- out_weight: bfloat16 [4096, 4096], P('head'), may hold values from -0.09375 to 0.09375
- selected: int32 [32, 6], replicated, may hold values from 0 to 255, as said below
Outputs:
- query_grad: bfloat16 [16384, 4096], P('seq', 'head')
- key_grad: bfloat16 [131072, 1024], P('seq', 'head')
- value_grad: bfloat16 [131072, 1024], P('seq', 'head')
The draws below stay inside these ranges and needn't reach their ends.
Inputs may be any that keep to these rules, and one draw needn't show every extreme that they name: `selected`: row i lists first the block i * 8 + 7, then 5 further distinct blocks of lower number; among them at most one lies in the run of 8 blocks j * 8 to j * 8 + 7 of any j other than i, and every row i >= 1 lists exactly one block of the run of j = 0.
All inputs are finite; a program needn't handle non-finite values.
Results may differ from the reference program's by a relative error of at most 0.0095.
Values may be sent and summed in bfloat16 or wider, within the bound.
A program may use at most 128 MiB of HBM per device.

```python
import jax
import jax.numpy as jnp
from jax import lax

D = 4096
HEADS = 32
KV_HEADS = 8
HEAD_DIM = 128
BLOCK = 512
TOPK = 6
KB_DEV = 8
QBLOCKS = 32
QUERIES = 16384
KBLOCKS = 256
KEYS = 131072


def draw_queries(key, part):
    noise = jax.random.normal(jax.random.fold_in(key, 11), (QUERIES, HEADS * HEAD_DIM), jnp.float32)
    base = jnp.clip(noise, -4.0, 4.0)
    return base.astype(jnp.bfloat16)


def draw_keys(key, part):
    noise = jax.random.normal(jax.random.fold_in(key, 13), (KEYS, KV_HEADS * HEAD_DIM), jnp.float32)
    base = jnp.clip(noise, -4.0, 4.0)
    return base.astype(jnp.bfloat16)


def draw_selected(key, part):
    row_count = QBLOCKS
    row_index = jnp.arange(row_count, dtype=jnp.int32)[:, None]
    owner_index = jnp.arange(row_count, dtype=jnp.int32)[None, :]
    offsets = jax.random.randint(jax.random.fold_in(key, 21), (row_count, row_count), 0, KB_DEV, dtype=jnp.int32)
    remote_blocks = owner_index * KB_DEV + offsets
    local_blocks = jnp.broadcast_to(row_index * KB_DEV + jnp.arange(KB_DEV - 1, dtype=jnp.int32)[None, :], (row_count, KB_DEV - 1))
    remote_draw = jax.random.randint(jax.random.fold_in(key, 22), (row_count, row_count), 0, 1024, dtype=jnp.int32)
    remote_draw = jnp.where(owner_index == 0, 2048, remote_draw)
    remote_score = jnp.where(owner_index < row_index, remote_draw, -1)
    local_score = jax.random.randint(jax.random.fold_in(key, 23), (row_count, KB_DEV - 1), 0, 256, dtype=jnp.int32)
    scores = jnp.concatenate([local_score, remote_score], axis=1)
    width_all = scores.shape[1]
    ranked = scores * width_all + jnp.arange(width_all, dtype=jnp.int32)[None, :]
    unused_values, chosen = lax.top_k(ranked, TOPK - 1)
    candidates = jnp.concatenate([local_blocks, remote_blocks], axis=1)
    picked = jnp.take_along_axis(candidates, chosen, axis=1)
    own_block = row_index * KB_DEV + KB_DEV - 1
    return jnp.concatenate([own_block, picked], axis=1).astype(jnp.int32)


def block_scale(own_key, dims, cuts, least, largest):
    level, own = 1.0, jax.random.fold_in(own_key, 6)
    for dim, shards_of in cuts:
        heights = jnp.exp(jax.random.uniform(jax.random.fold_in(own, dim), (shards_of,), jnp.float32, least / len(cuts), largest / len(cuts)))
        level = level * jnp.repeat(heights, dims[dim] // shards_of).reshape([-1 if axis == dim else 1 for axis in range(len(dims))])
    return level


def scatter_about(stream_key, dims, width, most, pieces=(), kind=jnp.bfloat16):
    result = width * jax.random.normal(stream_key, dims, jnp.float32)
    if pieces:
        result = result * block_scale(stream_key, dims, pieces, -0.22, 0.18)
    return jnp.clip(result, -most, most).astype(kind)


def setup_inputs(seed: int = 0) -> dict:
    streams_of = jax.random.split(jax.random.key(seed), 7)
    queries = draw_queries(jax.random.fold_in(streams_of[6], 71), 0)
    keys = draw_keys(jax.random.fold_in(streams_of[6], 71), 0)
    values = scatter_about(streams_of[2], (KEYS, KV_HEADS * HEAD_DIM), 1.0, 5.0, ((0, 32), (1, 4)))
    out_grad = scatter_about(streams_of[3], (QUERIES, D), 1.0, 6.0, ((0, 32), (1, 4)))
    out_weight = scatter_about(streams_of[4], (HEADS * HEAD_DIM, D), (HEADS * HEAD_DIM) ** -0.5, 0.09375, ((0, 4),))
    selected = draw_selected(jax.random.fold_in(streams_of[6], 71), 0)
    return {"queries": queries, "keys": keys, "values": values, "out_grad": out_grad, "out_weight": out_weight, "selected": selected}


def head_block(query_tile, grad_tile, key_tile, value_tile, visible):
    factor = HEAD_DIM ** -0.5
    query_f = query_tile.astype(jnp.float32)
    grad_f = grad_tile.astype(jnp.float32)
    key_f = key_tile.astype(jnp.float32)
    value_f = value_tile.astype(jnp.float32)
    scores = jnp.einsum("gqd,kd->gqk", query_f, key_f) * factor
    scores = jnp.where(visible, scores, -jnp.inf)
    row_max = jnp.max(scores, axis=-1, keepdims=True)
    shifted = jnp.exp(scores - row_max)
    weights = shifted / jnp.sum(shifted, axis=-1, keepdims=True)
    weights_low = lax.optimization_barrier(weights.astype(jnp.bfloat16)).astype(jnp.float32)
    attended = jnp.einsum("gqk,kd->gqd", weights_low, value_f)
    row_dot = jnp.sum(grad_f * attended, axis=-1, keepdims=True)
    value_part = jnp.einsum("gqk,gqd->kd", weights_low, grad_f)
    grad_weights = jnp.einsum("gqd,kd->gqk", grad_f, value_f)
    grad_scores = weights * (grad_weights - row_dot)
    grad_low = lax.optimization_barrier(grad_scores.astype(jnp.bfloat16)).astype(jnp.float32)
    query_part = jnp.einsum("gqk,kd->gqd", grad_low, key_f) * factor
    key_part = jnp.einsum("gqk,gqd->kd", grad_low, query_f) * factor
    return query_part, key_part, value_part


def reference(queries, keys, values, out_grad, out_weight, selected):
    group_size = HEADS // KV_HEADS
    grad_output = jnp.dot(out_grad, out_weight.T, preferred_element_type=jnp.float32).astype(jnp.bfloat16)
    key_tiles = keys.reshape(KBLOCKS, BLOCK, KV_HEADS, HEAD_DIM)
    value_tiles = values.reshape(KBLOCKS, BLOCK, KV_HEADS, HEAD_DIM)
    query_tiles = queries.reshape(QBLOCKS, BLOCK, KV_HEADS, group_size, HEAD_DIM)
    grad_tiles = grad_output.reshape(QBLOCKS, BLOCK, KV_HEADS, group_size, HEAD_DIM)
    length = TOPK * BLOCK
    column = jnp.arange(length, dtype=jnp.int32)[None, :]
    rowpos = jnp.arange(BLOCK, dtype=jnp.int32)[:, None]
    visible = (column >= BLOCK) | (column <= rowpos)

    def per_head(operands):
        query_tile, grad_tile, key_tile, value_tile = operands
        return head_block(query_tile, grad_tile, key_tile, value_tile, visible)

    def one_block(totals, number):
        key_sum, value_sum = totals
        chosen = lax.dynamic_index_in_dim(selected, number, 0, keepdims=False).astype(jnp.int32)
        key_pick = jnp.take(key_tiles, chosen, axis=0).reshape(length, KV_HEADS, HEAD_DIM)
        value_pick = jnp.take(value_tiles, chosen, axis=0).reshape(length, KV_HEADS, HEAD_DIM)
        query_block = lax.dynamic_index_in_dim(query_tiles, number, 0, keepdims=False)
        grad_block = lax.dynamic_index_in_dim(grad_tiles, number, 0, keepdims=False)
        query_part, key_part, value_part = lax.map(per_head, (query_block.transpose(1, 2, 0, 3), grad_block.transpose(1, 2, 0, 3), key_pick.transpose(1, 0, 2), value_pick.transpose(1, 0, 2)))
        query_out = query_part.transpose(2, 0, 1, 3).reshape(BLOCK, HEADS * HEAD_DIM).astype(jnp.bfloat16)
        key_low = lax.optimization_barrier(key_part.astype(jnp.bfloat16)).astype(jnp.float32)
        value_low = lax.optimization_barrier(value_part.astype(jnp.bfloat16)).astype(jnp.float32)
        key_add = key_low.transpose(1, 0, 2).reshape(TOPK, BLOCK, KV_HEADS, HEAD_DIM)
        value_add = value_low.transpose(1, 0, 2).reshape(TOPK, BLOCK, KV_HEADS, HEAD_DIM)
        key_sum = key_sum.at[chosen].add(key_add)
        value_sum = value_sum.at[chosen].add(value_add)
        return (key_sum, value_sum), query_out

    initial = (jnp.zeros((KBLOCKS, BLOCK, KV_HEADS, HEAD_DIM), jnp.float32), jnp.zeros((KBLOCKS, BLOCK, KV_HEADS, HEAD_DIM), jnp.float32))
    (key_sum, value_sum), query_rows = lax.scan(one_block, initial, jnp.arange(QBLOCKS, dtype=jnp.int32))
    query_grad = query_rows.reshape(QUERIES, HEADS * HEAD_DIM)
    key_grad = key_sum.reshape(KEYS, KV_HEADS * HEAD_DIM).astype(jnp.bfloat16)
    value_grad = value_sum.reshape(KEYS, KV_HEADS * HEAD_DIM).astype(jnp.bfloat16)
    return (query_grad, key_grad, value_grad)
```

```python
import functools
import math

import jax
import jax.numpy as jnp
from jax import lax
from jax.experimental import pallas as pl
from jax.experimental.pallas import tpu as pltpu
from jax.sharding import PartitionSpec as P

HEAD_DIM = 128
BLOCK = 512
TOPK = 6
SEQ = 32
ZDEV = 4
RUN = 8
PIECE = BLOCK // SEQ
SLOTS = TOPK - 1
KBLOCKS = SEQ * RUN
HEADS_HERE = 8
KV_HERE = 2
GROUP = HEADS_HERE // KV_HERE
FACTOR = HEAD_DIM**-0.5
EXP2_SCALE = FACTOR * math.log2(math.e)
MESH = pl.DeviceIdType.MESH

OFFSETS = [
    (1, 0), (3, 0), (0, 1), (0, 3), (1, 1), (3, 3), (1, 3), (3, 1),
    (2, 0), (0, 2), (1, 2), (3, 2), (2, 1), (2, 3), (2, 2),
]
DX_CODE = sum(dx * 4**t for t, (dx, _) in enumerate(OFFSETS))
DY_CODE = sum(dy * 4**t for t, (_, dy) in enumerate(OFFSETS))


def each_peer(me, visit):
    x, y, core = me // 8, me // 2 % 4, me % 2

    def step(flip, codes):
        dx_code, dy_code = codes
        peer = (x + dx_code % 4) % 4 * 8 + (y + dy_code % 4) % 4 * 2 + (core + flip) % 2
        visit(peer)
        return dx_code // 4, dy_code // 4

    for flip in (0, 1):
        lax.fori_loop(
            0,
            len(OFFSETS),
            lambda t, codes, flip=flip: step(flip, codes),
            (jnp.int32(DX_CODE), jnp.int32(DY_CODE)),
        )
    visit(x * 8 + y * 2 + 1 - core)


def dot_nt(a, b):
    return lax.dot_general(a, b, (((1,), (1,)), ((), ())), preferred_element_type=jnp.float32)


def dot_nn(a, b):
    return jnp.dot(a, b, preferred_element_type=jnp.float32)


def dot_tn(a, b):
    return lax.dot_general(a, b, (((0,), (0,)), ((), ())), preferred_element_type=jnp.float32)


def head_cols(index):
    return pl.ds(index * HEAD_DIM, HEAD_DIM)


def kernel(
    picks, table, q_hbm, k_hbm, v_hbm, og_hbm, w_hbm,
    dq_hbm, dk_hbm, dv_hbm,
    q_v, g_v, dq_v, og_v, pool_0, pool_1, stage, kv, acc, piece, came, running, total, home, stats,
    in_send, in_recv, pick_send, pick_recv, back_send, back_recv, home_send, home_recv,
    og_send, og_recv, self_in, self_move, load_sem, out_sem,
):
    me = lax.axis_index("seq")
    z = lax.axis_index("head")
    pool = (pool_0, pool_1)

    def remote(src, dst, send_sem, recv_sem, peer, peer_z=None):
        pltpu.make_async_remote_copy(
            src_ref=src, dst_ref=dst, send_sem=send_sem, recv_sem=recv_sem,
            device_id=(peer, z if peer_z is None else peer_z), device_id_type=MESH,
        ).start()

    def wait_for(ref, sem):
        pltpu.make_async_copy(ref, ref, sem).wait()

    loads = []

    def load(src, dst):
        copy = pltpu.make_async_copy(src, dst, load_sem.at[len(loads)])
        copy.start()
        loads.append(copy)

    load(og_hbm, og_v.at[z])
    for head in range(HEADS_HERE):
        load(q_hbm.at[:, head_cols(head)], q_v.at[head])
    for c in range(KV_HERE):
        for a, ref in enumerate((k_hbm, v_hbm)):
            load(ref.at[RUN - 1, :, :, head_cols(c)], kv.at[c, a, 0])

    barrier = pltpu.get_barrier_semaphore()

    def greet(t, carry):
        pl.semaphore_signal(
            barrier, inc=1, device_id=((me + t) % SEQ, z), device_id_type=MESH
        )
        return carry

    lax.fori_loop(1, SEQ, greet, 0)
    for t in range(1, ZDEV):
        pl.semaphore_signal(barrier, inc=1, device_id=(me, (z + t) % ZDEV), device_id_type=MESH)
    pl.semaphore_wait(barrier, SEQ - 1 + ZDEV - 1)

    for t in (1, 3, 2):
        remote(og_hbm, og_v.at[z], og_send, og_recv, me, (z + t) % ZDEV)

    def send_in(c, a):
        ref = (k_hbm, v_hbm)[a]
        pltpu.make_async_copy(
            ref.at[:, me, :, head_cols(c)], pool[c].at[a, pl.ds(me * RUN, RUN)], self_in.at[c, a]
        ).start()
        each_peer(
            me,
            lambda peer: remote(
                ref.at[:, peer, :, head_cols(c)],
                pool[c].at[a, pl.ds(me * RUN, RUN)],
                in_send.at[c], in_recv.at[c], peer,
            ),
        )

    def wait_in(c):
        others = pool[c].at[:, pl.ds(0, (SEQ - 1) * RUN)]
        wait_for(others, in_recv.at[c])
        wait_for(others, in_send.at[c])
        for a in range(2):
            wait_for(pool[c].at[a, pl.ds(0, RUN)], self_in.at[c, a])

    def send_picks(c):
        def choose(i, carry):
            for r in range(SLOTS):
                block = picks[i, r + 1]
                for a in range(2):
                    stage[c, i, a, r] = pool[c][a, block]
            return carry

        lax.fori_loop(0, SEQ, choose, 0)
        pltpu.make_async_copy(
            stage.at[c, me], kv.at[c, :, pl.ds(1, SLOTS), me], self_move.at[0, c]
        ).start()
        each_peer(
            me,
            lambda peer: remote(
                stage.at[c, peer], kv.at[c, :, pl.ds(1, SLOTS), me],
                pick_send.at[c], pick_recv.at[c], peer,
            ),
        )

    def wait_picks(c):
        others = stage.at[c, pl.ds(0, SEQ - 1)]
        wait_for(others, pick_recv.at[c])
        wait_for(others, pick_send.at[c])
        wait_for(stage.at[c, 0], self_move.at[0, c])

    def send_back(c):
        for slot in range(TOPK):
            for a in range(2):
                value = acc[a, slot]
                if a == 0:
                    value = value * FACTOR
                piece[c, a, slot] = value.astype(jnp.bfloat16).reshape(SEQ, PIECE, HEAD_DIM)
        pltpu.make_async_copy(
            piece.at[c, :, pl.ds(1, SLOTS), me], came.at[c, me], self_move.at[1, c]
        ).start()
        each_peer(
            me,
            lambda peer: remote(
                piece.at[c, :, pl.ds(1, SLOTS), peer], came.at[c, me],
                back_send.at[c], back_recv.at[c], peer,
            ),
        )

    def send_home(c):
        others = came.at[c, pl.ds(0, SEQ - 1)]
        wait_for(others, back_recv.at[c])
        wait_for(others, back_send.at[c])
        wait_for(came.at[c, 0], self_move.at[1, c])
        running[0] = jnp.zeros_like(running[0])

        def add(i, carry):
            for r in range(SLOTS):
                number = i * SLOTS + r
                running[number + 1] = (
                    came[c, i, :, r].astype(jnp.float32) + running[table[number]]
                )
            return carry

        lax.fori_loop(0, SEQ, add, 0)

        def gather(j, carry):
            for k in range(RUN):
                block = j * RUN + k
                total[c, :, block] = running[table[SEQ * SLOTS + block]].astype(jnp.bfloat16)
            return carry

        lax.fori_loop(0, SEQ, gather, 0)
        pltpu.make_async_copy(
            total.at[c, :, pl.ds(me * RUN, RUN)], home.at[c, :, :, me], self_move.at[2, c]
        ).start()
        each_peer(
            me,
            lambda peer: remote(
                total.at[c, :, pl.ds(peer * RUN, RUN)], home.at[c, :, :, me],
                home_send.at[c], home_recv.at[c], peer,
            ),
        )

    def finish(c):
        others = total.at[c, :, pl.ds(0, (SEQ - 1) * RUN)]
        wait_for(others, home_recv.at[c])
        wait_for(others, home_send.at[c])
        wait_for(total.at[c, :, pl.ds(0, RUN)], self_move.at[2, c])
        for a, ref in enumerate((dk_hbm, dv_hbm)):
            own = home[c, a, RUN - 1].astype(jnp.float32) + piece[c, a, 0].astype(jnp.float32)
            home[c, a, RUN - 1] = own.astype(jnp.bfloat16)
            pltpu.make_async_copy(
                home.at[c, a], ref.at[:, :, :, head_cols(c)], out_sem.at[c, a]
            ).start()

    send_in(0, 0)
    send_in(0, 1)
    send_in(1, 0)

    def project(w_v):
        w_load = pltpu.make_async_copy(w_hbm, w_v, load_sem.at[len(loads)])
        w_load.start()
        wait_in(0)
        send_picks(0)
        send_in(1, 1)
        w_load.wait()
        for copy in loads:
            copy.wait()
        og_others = og_v.at[pl.ds(0, ZDEV - 1)]
        wait_for(og_others, og_recv)
        wait_for(og_others, og_send)
        depth = og_v.shape[2]
        half = depth // 2
        for pair in range(HEADS_HERE // 2):
            rows = pl.ds(pair * 2 * HEAD_DIM, 2 * HEAD_DIM)

            def add(t, result, rows=rows):
                part = pl.ds(pl.multiple_of(t % 2 * half, half), half)
                columns = pl.ds(pl.multiple_of(t * half, half), half)
                return result + dot_nt(og_v[t // 2, :, part], w_v[rows, columns])

            result = lax.fori_loop(
                0, 2 * ZDEV, add, jnp.zeros((BLOCK, 2 * HEAD_DIM), jnp.float32)
            )
            for k in range(2):
                g_v[pair * 2 + k] = result[:, k * HEAD_DIM : (k + 1) * HEAD_DIM].astype(jnp.bfloat16)

    pl.run_scoped(project, pltpu.VMEM(w_hbm.shape, jnp.bfloat16))
    wait_picks(0)

    def attend(p_s, dp_s):
        def one_head(head, carry):
            c = head // GROUP

            @pl.when(head == 2)
            def _():
                wait_in(1)
                send_picks(1)

            @pl.when(head == GROUP)
            def _():
                send_back(0)
                wait_picks(1)

            @pl.when(head == GROUP + 2)
            def _():
                send_home(0)

            @pl.when(head % GROUP == 0)
            def _():
                acc[...] = jnp.zeros_like(acc)

            query = q_v[head]
            grad = g_v[head]

            def tiles(slot):
                key = kv[c, 0, slot].reshape(BLOCK, HEAD_DIM)
                value = kv[c, 1, slot].reshape(BLOCK, HEAD_DIM)
                return key, value

            def forward(slot, state):
                key, value = tiles(slot)
                scores = dot_nt(key, query)
                if state is None:
                    key_at = lax.broadcasted_iota(jnp.int32, (BLOCK, BLOCK), 0)
                    query_at = lax.broadcasted_iota(jnp.int32, (BLOCK, BLOCK), 1)
                    scores = jnp.where(key_at <= query_at, scores, -jnp.inf)
                    top = jnp.max(scores, axis=0, keepdims=True)
                else:
                    top = jnp.maximum(state[0], jnp.max(scores, axis=0, keepdims=True))
                shifted = jnp.exp2((scores - top) * EXP2_SCALE)
                grad_weights = dot_nt(value, grad)
                p_s[slot] = shifted
                dp_s[slot] = grad_weights
                stats[slot] = top
                norm = jnp.sum(shifted, axis=0, keepdims=True)
                row_dot = jnp.sum(shifted * grad_weights, axis=0, keepdims=True)
                if state is not None:
                    shrink = jnp.exp2((state[0] - top) * EXP2_SCALE)
                    norm = norm + state[1] * shrink
                    row_dot = row_dot + state[2] * shrink
                return top, norm, row_dot

            state = forward(0, None)
            top, norm, row_dot = lax.fori_loop(1, TOPK, forward, state)
            inverse = 1.0 / norm
            row_dot = row_dot * inverse

            def backward(slot, query_part):
                key, _ = tiles(slot)
                weights = p_s[slot] * (jnp.exp2((stats[slot] - top) * EXP2_SCALE) * inverse)
                weights_low = weights.astype(jnp.bfloat16)
                grad_low = (weights * (dp_s[slot] - row_dot)).astype(jnp.bfloat16)
                acc[1, slot] += dot_nn(weights_low, grad)
                acc[0, slot] += dot_nn(grad_low, query)
                return query_part + dot_tn(key, grad_low)

            query_part = lax.fori_loop(
                0, TOPK, backward, jnp.zeros((HEAD_DIM, BLOCK), jnp.float32)
            )
            dq_v[head] = jnp.transpose(query_part * FACTOR).astype(jnp.bfloat16)
            return carry

        lax.fori_loop(0, HEADS_HERE, one_head, 0)

    pl.run_scoped(
        attend,
        pltpu.VMEM((TOPK, BLOCK, BLOCK), jnp.float32),
        pltpu.VMEM((TOPK, BLOCK, BLOCK), jnp.float32),
    )
    send_back(1)
    outs = []
    for head in range(HEADS_HERE):
        copy = pltpu.make_async_copy(
            dq_v.at[head], dq_hbm.at[:, head_cols(head)], load_sem.at[head]
        )
        copy.start()
        outs.append(copy)
    send_home(1)
    finish(0)
    finish(1)
    for copy in outs:
        copy.wait()
    for c in range(KV_HERE):
        for a, ref in enumerate((dk_hbm, dv_hbm)):
            pltpu.make_async_copy(
                home.at[c, a], ref.at[:, :, :, head_cols(c)], out_sem.at[c, a]
            ).wait()


def shards(queries, keys, values, out_grad, out_weight, selected):
    bf16, f32 = jnp.bfloat16, jnp.float32
    kv_cols = keys.shape[1]
    tiled = (RUN, SEQ, PIECE, kv_cols)
    listed = selected[:, 1:].reshape(-1)
    count = listed.shape[0]
    numbers = jnp.arange(count, dtype=jnp.int32)
    target = jnp.concatenate([listed, jnp.arange(KBLOCKS, dtype=jnp.int32)])
    limit = jnp.concatenate([numbers, jnp.full((KBLOCKS,), count, jnp.int32)])
    same = (target[:, None] == listed[None, :]) & (numbers[None, :] < limit[:, None])
    table = jnp.max(jnp.where(same, numbers[None, :] + 1, 0), axis=1)
    tile = (PIECE, HEAD_DIM)
    dma = pltpu.SemaphoreType.DMA
    hbm = pl.BlockSpec(memory_space=pltpu.HBM)
    smem = pl.BlockSpec(memory_space=pltpu.SMEM)
    query_grad, key_grad, value_grad = pl.pallas_call(
        kernel,
        out_shape=(
            jax.ShapeDtypeStruct(queries.shape, bf16),
            jax.ShapeDtypeStruct(tiled, bf16),
            jax.ShapeDtypeStruct(tiled, bf16),
        ),
        in_specs=[smem, smem, hbm, hbm, hbm, hbm, hbm],
        out_specs=(hbm, hbm, hbm),
        scratch_shapes=[
            pltpu.VMEM((HEADS_HERE, BLOCK, HEAD_DIM), bf16),
            pltpu.VMEM((HEADS_HERE, BLOCK, HEAD_DIM), bf16),
            pltpu.VMEM((HEADS_HERE, BLOCK, HEAD_DIM), bf16),
            pltpu.VMEM((ZDEV, *out_grad.shape), bf16),
            *[pltpu.VMEM((2, KBLOCKS, *tile), bf16)] * KV_HERE,
            pltpu.VMEM((KV_HERE, SEQ, 2, SLOTS, *tile), bf16),
            pltpu.VMEM((KV_HERE, 2, TOPK, SEQ, *tile), bf16),
            pltpu.VMEM((2, TOPK, BLOCK, HEAD_DIM), f32),
            pltpu.VMEM((KV_HERE, 2, TOPK, SEQ, *tile), bf16),
            pltpu.VMEM((KV_HERE, SEQ, 2, SLOTS, *tile), bf16),
            pltpu.VMEM((SEQ * SLOTS + 1, 2, *tile), f32),
            pltpu.VMEM((KV_HERE, 2, KBLOCKS, *tile), bf16),
            pltpu.VMEM((KV_HERE, 2, RUN, SEQ, *tile), bf16),
            pltpu.VMEM((TOPK, 1, BLOCK), f32),
            *[dma((KV_HERE,))] * 8,
            dma, dma,
            dma((KV_HERE, 2)),
            dma((3, KV_HERE)),
            dma((HEADS_HERE + 6,)),
            dma((KV_HERE, 2)),
        ],
        compiler_params=pltpu.CompilerParams(
            collective_id=0, has_side_effects=True, vmem_limit_bytes=62 << 20
        ),
    )(
        selected, table, queries, keys.reshape(tiled), values.reshape(tiled), out_grad, out_weight
    )
    return query_grad, key_grad.reshape(keys.shape), value_grad.reshape(values.shape)


def solution(mesh):
    in_specs = (
        P("seq", "head"),
        P("seq", "head"),
        P("seq", "head"),
        P("seq", "head"),
        P("head", None),
        P(),
    )
    out_specs = (P("seq", "head"), P("seq", "head"), P("seq", "head"))
    return jax.shard_map(shards, mesh=mesh, in_specs=in_specs, out_specs=out_specs, check_vma=False)
```

```python
import functools
import math

import jax
import jax.numpy as jnp
from jax import lax
from jax.experimental import pallas as pl
from jax.experimental.pallas import tpu as pltpu
from jax.sharding import PartitionSpec as P

HEAD_DIM = 128
BLOCK = 512
TOPK = 6
SEQ = 32
ZDEV = 4
RUN = 8
PIECE = BLOCK // SEQ
SLOTS = TOPK - 1
KBLOCKS = SEQ * RUN
TABLE = 512
HEADS_HERE = 8
KV_HERE = 2
GROUP = HEADS_HERE // KV_HERE
FACTOR = HEAD_DIM**-0.5
EXP2_SCALE = FACTOR * math.log2(math.e)
MESH = pl.DeviceIdType.MESH

OFFSETS = [
    (1, 0), (3, 0), (0, 1), (0, 3), (1, 1), (3, 3), (1, 3), (3, 1),
    (2, 0), (0, 2), (1, 2), (3, 2), (2, 1), (2, 3), (2, 2),
]
DX_CODE = sum(dx * 4**t for t, (dx, _) in enumerate(OFFSETS))
DY_CODE = sum(dy * 4**t for t, (_, dy) in enumerate(OFFSETS))


def each_peer(me, visit):
    x, y, core = me // 8, me // 2 % 4, me % 2

    def step(flip, codes):
        dx_code, dy_code = codes
        peer = (x + dx_code % 4) % 4 * 8 + (y + dy_code % 4) % 4 * 2 + (core + flip) % 2
        visit(peer)
        return dx_code // 4, dy_code // 4

    for flip in (0, 1):
        lax.fori_loop(
            0,
            len(OFFSETS),
            lambda t, codes, flip=flip: step(flip, codes),
            (jnp.int32(DX_CODE), jnp.int32(DY_CODE)),
        )
    visit(x * 8 + y * 2 + 1 - core)


def dot_nt(a, b):
    return lax.dot_general(a, b, (((1,), (1,)), ((), ())), preferred_element_type=jnp.float32)


def dot_nn(a, b):
    return jnp.dot(a, b, preferred_element_type=jnp.float32)


def dot_tn(a, b):
    return lax.dot_general(a, b, (((0,), (0,)), ((), ())), preferred_element_type=jnp.float32)


def head_cols(index):
    return pl.ds(index * HEAD_DIM, HEAD_DIM)


def kernel(
    selected, q_hbm, k_hbm, v_hbm, og_hbm, w_hbm,
    dq_out, dk_out, dv_out,
    selected_v, table_v, table, q_v, g_v, og_v, pool_0, pool_1, pool_2, pool_3, stage, kv, acc, piece, came,
    running, total, stats,
    in_send, in_recv, pick_send, pick_recv, back_send, back_recv, home_send, home_recv,
    og_send, og_recv, self_move, load_sem, table_sem,
):
    me = lax.axis_index("seq")
    z = lax.axis_index("head")
    pool = ((pool_0, pool_1), (pool_2, pool_3))

    def remote(src, dst, send_sem, recv_sem, peer, peer_z=None):
        pltpu.make_async_remote_copy(
            src_ref=src, dst_ref=dst, send_sem=send_sem, recv_sem=recv_sem,
            device_id=(peer, z if peer_z is None else peer_z), device_id_type=MESH,
        ).start()

    def wait_for(ref, sem):
        pltpu.make_async_copy(ref, ref, sem).wait()

    table_load = pltpu.make_async_copy(selected, selected_v, table_sem)
    table_load.start()
    loads = []

    def load(src, dst):
        copy = pltpu.make_async_copy(src, dst, load_sem.at[len(loads)])
        copy.start()
        loads.append(copy)

    load(og_hbm, og_v.at[z])
    for head in range(HEADS_HERE):
        load(q_hbm.at[:, head_cols(head)], q_v.at[head])
    for c in range(KV_HERE):
        for a, ref in enumerate((k_hbm, v_hbm)):
            load(ref.at[RUN - 1, :, :, head_cols(c)], kv.at[c, a, 0])

    barrier = pltpu.get_barrier_semaphore()

    def greet(t, carry):
        pl.semaphore_signal(
            barrier, inc=1, device_id=((me + t) % SEQ, z), device_id_type=MESH
        )
        return carry

    lax.fori_loop(1, SEQ, greet, 0)
    for t in range(1, ZDEV):
        pl.semaphore_signal(barrier, inc=1, device_id=(me, (z + t) % ZDEV), device_id_type=MESH)
    pl.semaphore_wait(barrier, SEQ - 1 + ZDEV - 1)

    above, below = (z + 1) % ZDEV, (z + ZDEV - 1) % ZDEV
    remote(og_hbm, og_v.at[z], og_send.at[0], og_recv.at[0], me, above)
    remote(og_hbm, og_v.at[z], og_send.at[1], og_recv.at[1], me, below)

    def relay_cotangent():
        half = og_v.shape[1] // 2
        for way, (source, target) in enumerate(((below, above), (above, below))):
            wait_for(og_v.at[source], og_recv.at[way])
            part = og_v.at[source, pl.ds(way * half, half)]
            remote(part, part, og_send.at[2 + way], og_recv.at[2 + way], me, target)

    def wait_cotangent():
        half = og_v.at[0, pl.ds(0, og_v.shape[1] // 2)]
        for way in range(2):
            wait_for(og_v.at[0], og_send.at[way])
            wait_for(half, og_send.at[2 + way])
            wait_for(half, og_recv.at[2 + way])

    def send_in(c, a):
        ref = (k_hbm, v_hbm)[a]
        mine = pool[c][a].at[pl.ds(me * RUN, RUN)]
        pltpu.make_async_copy(
            ref.at[:, me, :, head_cols(c)], mine, self_move.at[0, c, a]
        ).start()
        each_peer(
            me,
            lambda peer: remote(
                ref.at[:, peer, :, head_cols(c)], mine,
                in_send.at[c, a], in_recv.at[c, a], peer,
            ),
        )

    def send_picks(c, a):
        others = pool[c][a].at[pl.ds(0, (SEQ - 1) * RUN)]
        wait_for(others, in_recv.at[c, a])
        wait_for(others, in_send.at[c, a])
        wait_for(pool[c][a].at[pl.ds(0, RUN)], self_move.at[0, c, a])

        def choose(i, carry):
            for r in range(SLOTS):
                stage[c, a, i, r] = pool[c][a][table[0, i * SLOTS + r]]
            return carry

        lax.fori_loop(0, SEQ, choose, 0)
        mine = kv.at[c, a, pl.ds(1, SLOTS), me]
        pltpu.make_async_copy(stage.at[c, a, me], mine, self_move.at[1, c, a]).start()
        each_peer(
            me,
            lambda peer: remote(
                stage.at[c, a, peer], mine, pick_send.at[c, a], pick_recv.at[c, a], peer
            ),
        )

    def wait_picks(c, a):
        others = stage.at[c, a, pl.ds(0, SEQ - 1)]
        wait_for(others, pick_recv.at[c, a])
        wait_for(others, pick_send.at[c, a])
        wait_for(stage.at[c, a, 0], self_move.at[1, c, a])

    def send_back(c, a):
        for slot in range(TOPK):
            value = acc[a, slot]
            if a == 0:
                value = value * FACTOR
            piece[c, a, slot] = value.astype(jnp.bfloat16).reshape(SEQ, PIECE, HEAD_DIM)
        mine = came.at[c, a, me]
        pltpu.make_async_copy(
            piece.at[c, a, pl.ds(1, SLOTS), me], mine, self_move.at[2, c, a]
        ).start()
        each_peer(
            me,
            lambda peer: remote(
                piece.at[c, a, pl.ds(1, SLOTS), peer], mine,
                back_send.at[c, a], back_recv.at[c, a], peer,
            ),
        )

    def send_home(c, a):
        others = came.at[c, a, pl.ds(0, SEQ - 1)]
        wait_for(others, back_recv.at[c, a])
        wait_for(others, back_send.at[c, a])
        wait_for(came.at[c, a, 0], self_move.at[2, c, a])
        running[0] = jnp.zeros_like(running[0])

        def add(i, carry):
            for r in range(SLOTS):
                number = i * SLOTS + r
                running[number + 1] = (
                    came[c, a, i, r].astype(jnp.float32) + running[table[1, number]]
                )
            return carry

        lax.fori_loop(0, SEQ, add, 0)

        def gather(j, carry):
            for k in range(RUN):
                block = j * RUN + k
                total[c, a, block] = running[table[1, SEQ * SLOTS + block]].astype(jnp.bfloat16)
            return carry

        lax.fori_loop(0, SEQ, gather, 0)
        mine = (dk_out, dv_out)[a].at[:, me, :, head_cols(c)]
        pltpu.make_async_copy(
            total.at[c, a, pl.ds(me * RUN, RUN)], mine, self_move.at[3, c, a]
        ).start()
        each_peer(
            me,
            lambda peer: remote(
                total.at[c, a, pl.ds(peer * RUN, RUN)], mine,
                home_send.at[c, a], home_recv.at[c, a], peer,
            ),
        )

    def finish(c, a):
        others = total.at[c, a, pl.ds(0, (SEQ - 1) * RUN)]
        wait_for(others, home_recv.at[c, a])
        wait_for(others, home_send.at[c, a])
        wait_for(total.at[c, a, pl.ds(0, RUN)], self_move.at[3, c, a])
        ref, columns = (dk_out, dv_out)[a], head_cols(c)
        own = ref[RUN - 1, :, :, columns].astype(jnp.float32)
        own = own + piece[c, a, 0].astype(jnp.float32)
        ref[RUN - 1, :, :, columns] = own.astype(jnp.bfloat16)

    def make_table():
        table_load.wait()
        rows_of = jnp.transpose(selected_v[...])
        lane = lax.broadcasted_iota(jnp.int32, (SEQ, table_v.shape[1]), 1)
        row = lax.broadcasted_iota(jnp.int32, (SEQ, table_v.shape[1]), 0)
        count = SEQ * SLOTS
        listed = jnp.zeros_like(lane)
        for r in range(SLOTS):
            listed += jnp.where(lane == row * SLOTS + r, rows_of[:, r + 1 : r + 2], 0)
        listed = jnp.sum(listed, axis=0, keepdims=True)
        target = jnp.where(lane < count, listed, lane - count)
        limit = jnp.minimum(lane, count)
        latest = jnp.zeros_like(lane)
        for r in range(SLOTS):
            number = row * SLOTS + r
            same = (rows_of[:, r + 1 : r + 2] == target) & (number < limit)
            latest = jnp.maximum(latest, jnp.where(same, number + 1, 0))
        table_v[0:1, :] = listed
        table_v[1:2, :] = jnp.max(latest, axis=0, keepdims=True)
        table_store = pltpu.make_async_copy(table_v, table, table_sem)
        table_store.start()
        table_store.wait()

    send_in(0, 0)
    send_in(0, 1)
    make_table()

    def project(w_v):
        w_load = pltpu.make_async_copy(w_hbm, w_v, load_sem.at[len(loads)])
        w_load.start()
        send_picks(0, 0)
        relay_cotangent()
        send_picks(0, 1)
        send_in(1, 0)
        send_in(1, 1)
        w_load.wait()
        for copy in loads:
            copy.wait()
        wait_cotangent()
        depth = og_v.shape[2]
        half = depth // 2
        for pair in range(HEADS_HERE // 2):
            rows = pl.ds(pair * 2 * HEAD_DIM, 2 * HEAD_DIM)

            def add(t, result, rows=rows):
                part = pl.ds(pl.multiple_of(t % 2 * half, half), half)
                columns = pl.ds(pl.multiple_of(t * half, half), half)
                return result + dot_nt(og_v[t // 2, :, part], w_v[rows, columns])

            result = lax.fori_loop(
                0, 2 * ZDEV, add, jnp.zeros((BLOCK, 2 * HEAD_DIM), jnp.float32)
            )
            for k in range(2):
                g_v[pair * 2 + k] = result[:, k * HEAD_DIM : (k + 1) * HEAD_DIM].astype(jnp.bfloat16)

    pl.run_scoped(project, pltpu.VMEM(w_hbm.shape, jnp.bfloat16))
    wait_picks(0, 0)
    wait_picks(0, 1)

    def attend(p_s, dp_s):
        def one_head(head, carry):
            c = head // GROUP

            @pl.when(head == 1)
            def _():
                send_picks(1, 0)

            @pl.when(head == 3)
            def _():
                send_picks(1, 1)

            @pl.when(head == GROUP)
            def _():
                send_back(0, 0)
                send_back(0, 1)
                wait_picks(1, 0)
                wait_picks(1, 1)

            @pl.when(head == GROUP + 1)
            def _():
                send_home(0, 0)

            @pl.when(head == GROUP + 2)
            def _():
                send_home(0, 1)

            @pl.when(head % GROUP == 0)
            def _():
                acc[...] = jnp.zeros_like(acc)

            query = q_v[head]
            grad = g_v[head]

            def tiles(slot):
                key = kv[c, 0, slot].reshape(BLOCK, HEAD_DIM)
                value = kv[c, 1, slot].reshape(BLOCK, HEAD_DIM)
                return key, value

            def forward(slot, state):
                key, value = tiles(slot)
                scores = dot_nt(key, query)
                if state is None:
                    key_at = lax.broadcasted_iota(jnp.int32, (BLOCK, BLOCK), 0)
                    query_at = lax.broadcasted_iota(jnp.int32, (BLOCK, BLOCK), 1)
                    scores = jnp.where(key_at <= query_at, scores, -jnp.inf)
                    top = jnp.max(scores, axis=0, keepdims=True)
                else:
                    top = jnp.maximum(state[0], jnp.max(scores, axis=0, keepdims=True))
                shifted = jnp.exp2((scores - top) * EXP2_SCALE)
                grad_weights = dot_nt(value, grad)
                p_s[slot] = shifted
                dp_s[slot] = grad_weights
                stats[slot] = top
                norm = jnp.sum(shifted, axis=0, keepdims=True)
                row_dot = jnp.sum(shifted * grad_weights, axis=0, keepdims=True)
                if state is not None:
                    shrink = jnp.exp2((state[0] - top) * EXP2_SCALE)
                    norm = norm + state[1] * shrink
                    row_dot = row_dot + state[2] * shrink
                return top, norm, row_dot

            state = forward(0, None)
            top, norm, row_dot = lax.fori_loop(1, TOPK, forward, state)
            inverse = 1.0 / norm
            row_dot = row_dot * inverse

            def backward(slot, query_part):
                key, _ = tiles(slot)
                weights = p_s[slot] * (jnp.exp2((stats[slot] - top) * EXP2_SCALE) * inverse)
                weights_low = weights.astype(jnp.bfloat16)
                grad_low = (weights * (dp_s[slot] - row_dot)).astype(jnp.bfloat16)
                acc[1, slot] += dot_nn(weights_low, grad)
                acc[0, slot] += dot_nn(grad_low, query)
                return query_part + dot_tn(key, grad_low)

            query_part = lax.fori_loop(
                0, TOPK, backward, jnp.zeros((HEAD_DIM, BLOCK), jnp.float32)
            )
            columns = pl.ds(pl.multiple_of(head * HEAD_DIM, HEAD_DIM), HEAD_DIM)
            dq_out[:, columns] = jnp.transpose(query_part * FACTOR).astype(jnp.bfloat16)
            return carry

        lax.fori_loop(0, HEADS_HERE, one_head, 0)

    pl.run_scoped(
        attend,
        pltpu.VMEM((TOPK, BLOCK, BLOCK), jnp.float32),
        pltpu.VMEM((TOPK, BLOCK, BLOCK), jnp.float32),
    )
    send_back(1, 0)
    send_back(1, 1)
    send_home(1, 0)
    send_home(1, 1)
    for c in range(KV_HERE):
        for a in range(2):
            finish(c, a)


def shards(queries, keys, values, out_grad, out_weight, selected):
    bf16, f32 = jnp.bfloat16, jnp.float32
    kv_cols = keys.shape[1]
    tiled = (RUN, SEQ, PIECE, kv_cols)
    tile = (PIECE, HEAD_DIM)
    dma = pltpu.SemaphoreType.DMA
    hbm = pl.BlockSpec(memory_space=pltpu.HBM)
    vmem = pl.BlockSpec(memory_space=pltpu.VMEM)
    query_grad, key_grad, value_grad = pl.pallas_call(
        kernel,
        out_shape=(
            jax.ShapeDtypeStruct(queries.shape, bf16),
            jax.ShapeDtypeStruct(tiled, bf16),
            jax.ShapeDtypeStruct(tiled, bf16),
        ),
        in_specs=[hbm] * 6,
        out_specs=(vmem, vmem, vmem),
        scratch_shapes=[
            pltpu.VMEM(selected.shape[::-1], jnp.int32),
            pltpu.VMEM((2, TABLE), jnp.int32),
            pltpu.SMEM((2, TABLE), jnp.int32),
            pltpu.VMEM((HEADS_HERE, BLOCK, HEAD_DIM), bf16),
            pltpu.VMEM((HEADS_HERE, BLOCK, HEAD_DIM), bf16),
            pltpu.VMEM((ZDEV, *out_grad.shape), bf16),
            *[pltpu.VMEM((KBLOCKS, *tile), bf16)] * 2 * KV_HERE,
            pltpu.VMEM((KV_HERE, 2, SEQ, SLOTS, *tile), bf16),
            pltpu.VMEM((KV_HERE, 2, TOPK, SEQ, *tile), bf16),
            pltpu.VMEM((2, TOPK, BLOCK, HEAD_DIM), f32),
            pltpu.VMEM((KV_HERE, 2, TOPK, SEQ, *tile), bf16),
            pltpu.VMEM((KV_HERE, 2, SEQ, SLOTS, *tile), bf16),
            pltpu.VMEM((SEQ * SLOTS + 1, *tile), f32),
            pltpu.VMEM((KV_HERE, 2, KBLOCKS, *tile), bf16),
            pltpu.VMEM((TOPK, 1, BLOCK), f32),
            *[dma((KV_HERE, 2))] * 8,
            dma((4,)),
            dma((4,)),
            dma((4, KV_HERE, 2)),
            dma((HEADS_HERE + 6,)),
            dma,
        ],
        compiler_params=pltpu.CompilerParams(
            collective_id=0, has_side_effects=True, vmem_limit_bytes=62 << 20
        ),
    )(
        selected.T, queries, keys.reshape(tiled), values.reshape(tiled), out_grad, out_weight
    )
    return query_grad, key_grad.reshape(keys.shape), value_grad.reshape(values.shape)


def solution(mesh):
    in_specs = (
        P("seq", "head"),
        P("seq", "head"),
        P("seq", "head"),
        P("seq", "head"),
        P("head", None),
        P(),
    )
    out_specs = (P("seq", "head"), P("seq", "head"), P("seq", "head"))
    return jax.shard_map(shards, mesh=mesh, in_specs=in_specs, out_specs=out_specs, check_vma=False)
```

```python
import functools
import math

import jax
import jax.numpy as jnp
from jax import lax
from jax.experimental import pallas as pl
from jax.experimental.pallas import tpu as pltpu
from jax.sharding import PartitionSpec as P

HEAD_DIM = 128
BLOCK = 512
TOPK = 6
SEQ = 32
ZDEV = 4
RUN = 8
PIECE = BLOCK // SEQ
SLOTS = TOPK - 1
KBLOCKS = SEQ * RUN
TABLE = 512
HEADS_HERE = 8
KV_HERE = 2
GROUP = HEADS_HERE // KV_HERE
FACTOR = HEAD_DIM**-0.5
EXP2_SCALE = FACTOR * math.log2(math.e)
MESH = pl.DeviceIdType.MESH

OFFSETS = [
    (2, 2), (1, 2), (2, 1), (3, 2), (2, 3), (1, 1), (3, 3), (1, 3),
    (3, 1), (2, 0), (0, 2), (1, 0), (3, 0), (0, 1), (0, 3),
]
DX_CODE = sum(dx * 4**t for t, (dx, _) in enumerate(OFFSETS))
DY_CODE = sum(dy * 4**t for t, (_, dy) in enumerate(OFFSETS))


def each_peer(me, visit):
    x, y, core = me // 8, me // 2 % 4, me % 2

    def step(flip, codes):
        dx_code, dy_code = codes
        peer = (x + dx_code % 4) % 4 * 8 + (y + dy_code % 4) % 4 * 2 + (core + flip) % 2
        visit(peer)
        return dx_code // 4, dy_code // 4

    for flip in (0, 1):
        lax.fori_loop(
            0,
            len(OFFSETS),
            lambda t, codes, flip=flip: step(flip, codes),
            (DX_CODE + core * (DY_CODE - DX_CODE), DY_CODE + core * (DX_CODE - DY_CODE)),
        )
    visit(x * 8 + y * 2 + 1 - core)


def dot_nt(a, b):
    return lax.dot_general(a, b, (((1,), (1,)), ((), ())), preferred_element_type=jnp.float32)


def dot_nn(a, b):
    return jnp.dot(a, b, preferred_element_type=jnp.float32)


def dot_tn(a, b):
    return lax.dot_general(a, b, (((0,), (0,)), ((), ())), preferred_element_type=jnp.float32)


def head_cols(index):
    return pl.ds(index * HEAD_DIM, HEAD_DIM)


def kernel(
    selected, q_hbm, k_hbm, v_hbm, og_hbm, w_hbm,
    dq_out, dk_out, dv_out,
    selected_v, table_v, table, q_v, g_v, og_v, pool_0, pool_1, pool_2, pool_3, stage, kv, acc, piece, came,
    running, total, stats,
    in_send, in_recv, pick_send, pick_recv, back_send, back_recv, home_send, home_recv,
    og_send, og_recv, self_move, load_sem, table_sem,
):
    me = lax.axis_index("seq")
    z = lax.axis_index("head")
    pool = ((pool_0, pool_1), (pool_2, pool_3))

    def remote(src, dst, send_sem, recv_sem, peer, peer_z=None):
        pltpu.make_async_remote_copy(
            src_ref=src, dst_ref=dst, send_sem=send_sem, recv_sem=recv_sem,
            device_id=(peer, z if peer_z is None else peer_z), device_id_type=MESH,
        ).start()

    def wait_for(ref, sem):
        pltpu.make_async_copy(ref, ref, sem).wait()

    table_load = pltpu.make_async_copy(selected, selected_v, table_sem)
    table_load.start()
    loads = []

    def load(src, dst):
        copy = pltpu.make_async_copy(src, dst, load_sem.at[len(loads)])
        copy.start()
        loads.append(copy)

    load(og_hbm, og_v.at[z])
    for head in range(HEADS_HERE):
        load(q_hbm.at[:, head_cols(head)], q_v.at[head])
    for c in range(KV_HERE):
        for a, ref in enumerate((k_hbm, v_hbm)):
            load(ref.at[RUN - 1, :, :, head_cols(c)], kv.at[c, a, 0])

    barrier = pltpu.get_barrier_semaphore()

    def greet(t, carry):
        pl.semaphore_signal(
            barrier, inc=1, device_id=((me + t) % SEQ, z), device_id_type=MESH
        )
        return carry

    lax.fori_loop(1, SEQ, greet, 0)
    for t in range(1, ZDEV):
        pl.semaphore_signal(barrier, inc=1, device_id=(me, (z + t) % ZDEV), device_id_type=MESH)
    pl.semaphore_wait(barrier, SEQ - 1 + ZDEV - 1)

    above, below = (z + 1) % ZDEV, (z + ZDEV - 1) % ZDEV
    remote(og_hbm, og_v.at[z], og_send.at[0], og_recv.at[0], me, above)
    remote(og_hbm, og_v.at[z], og_send.at[1], og_recv.at[1], me, below)

    def relay_cotangent():
        half = og_v.shape[1] // 2
        for way, (source, target) in enumerate(((below, above), (above, below))):
            wait_for(og_v.at[source], og_recv.at[way])
            part = og_v.at[source, pl.ds(way * half, half)]
            remote(part, part, og_send.at[2 + way], og_recv.at[2 + way], me, target)

    def wait_cotangent():
        half = og_v.at[0, pl.ds(0, og_v.shape[1] // 2)]
        for way in range(2):
            wait_for(og_v.at[0], og_send.at[way])
            wait_for(half, og_send.at[2 + way])
            wait_for(half, og_recv.at[2 + way])

    def send_in(c, a):
        ref = (k_hbm, v_hbm)[a]
        mine = pool[c][a].at[pl.ds(me * RUN, RUN)]
        pltpu.make_async_copy(
            ref.at[:, me, :, head_cols(c)], mine, self_move.at[0, c, a]
        ).start()
        each_peer(
            me,
            lambda peer: remote(
                ref.at[:, peer, :, head_cols(c)], mine,
                in_send.at[c, a], in_recv.at[c, a], peer,
            ),
        )

    def send_picks(c, a):
        others = pool[c][a].at[pl.ds(0, (SEQ - 1) * RUN)]
        wait_for(others, in_recv.at[c, a])
        wait_for(others, in_send.at[c, a])
        wait_for(pool[c][a].at[pl.ds(0, RUN)], self_move.at[0, c, a])

        def choose(i, carry):
            for r in range(SLOTS):
                stage[c, a, i, r] = pool[c][a][table[0, i * SLOTS + r]]
            return carry

        lax.fori_loop(0, SEQ, choose, 0)
        mine = kv.at[c, a, pl.ds(1, SLOTS), me]
        pltpu.make_async_copy(stage.at[c, a, me], mine, self_move.at[1, c, a]).start()
        each_peer(
            me,
            lambda peer: remote(
                stage.at[c, a, peer], mine, pick_send.at[c, a], pick_recv.at[c, a], peer
            ),
        )

    def wait_picks(c, a):
        others = stage.at[c, a, pl.ds(0, SEQ - 1)]
        wait_for(others, pick_recv.at[c, a])
        wait_for(others, pick_send.at[c, a])
        wait_for(stage.at[c, a, 0], self_move.at[1, c, a])

    def send_back(c, a):
        for slot in range(TOPK):
            value = acc[a, slot]
            if a == 0:
                value = value * FACTOR
            piece[c, a, slot] = value.astype(jnp.bfloat16).reshape(SEQ, PIECE, HEAD_DIM)
        mine = came.at[c, a, me]
        pltpu.make_async_copy(
            piece.at[c, a, pl.ds(1, SLOTS), me], mine, self_move.at[2, c, a]
        ).start()
        each_peer(
            me,
            lambda peer: remote(
                piece.at[c, a, pl.ds(1, SLOTS), peer], mine,
                back_send.at[c, a], back_recv.at[c, a], peer,
            ),
        )

    def send_home(c, a):
        others = came.at[c, a, pl.ds(0, SEQ - 1)]
        wait_for(others, back_recv.at[c, a])
        wait_for(others, back_send.at[c, a])
        wait_for(came.at[c, a, 0], self_move.at[2, c, a])
        running[0] = jnp.zeros_like(running[0])

        def add(i, carry):
            for r in range(SLOTS):
                number = i * SLOTS + r
                running[number + 1] = (
                    came[c, a, i, r].astype(jnp.float32) + running[table[1, number]]
                )
            return carry

        lax.fori_loop(0, SEQ, add, 0)

        def gather(j, carry):
            for k in range(RUN):
                block = j * RUN + k
                total[c, a, block] = running[table[1, SEQ * SLOTS + block]].astype(jnp.bfloat16)
            return carry

        lax.fori_loop(0, SEQ, gather, 0)
        mine = (dk_out, dv_out)[a].at[:, me, :, head_cols(c)]
        pltpu.make_async_copy(
            total.at[c, a, pl.ds(me * RUN, RUN)], mine, self_move.at[3, c, a]
        ).start()
        each_peer(
            me,
            lambda peer: remote(
                total.at[c, a, pl.ds(peer * RUN, RUN)], mine,
                home_send.at[c, a], home_recv.at[c, a], peer,
            ),
        )

    def finish(c, a):
        others = total.at[c, a, pl.ds(0, (SEQ - 1) * RUN)]
        wait_for(others, home_recv.at[c, a])
        wait_for(others, home_send.at[c, a])
        wait_for(total.at[c, a, pl.ds(0, RUN)], self_move.at[3, c, a])
        ref, columns = (dk_out, dv_out)[a], head_cols(c)
        own = ref[RUN - 1, :, :, columns].astype(jnp.float32)
        own = own + piece[c, a, 0].astype(jnp.float32)
        ref[RUN - 1, :, :, columns] = own.astype(jnp.bfloat16)

    def make_table():
        table_load.wait()
        rows_of = jnp.transpose(selected_v[...])
        lane = lax.broadcasted_iota(jnp.int32, (SEQ, table_v.shape[1]), 1)
        row = lax.broadcasted_iota(jnp.int32, (SEQ, table_v.shape[1]), 0)
        count = SEQ * SLOTS
        listed = jnp.zeros_like(lane)
        for r in range(SLOTS):
            listed += jnp.where(lane == row * SLOTS + r, rows_of[:, r + 1 : r + 2], 0)
        listed = jnp.sum(listed, axis=0, keepdims=True)
        target = jnp.where(lane < count, listed, lane - count)
        limit = jnp.minimum(lane, count)
        latest = jnp.zeros_like(lane)
        for r in range(SLOTS):
            number = row * SLOTS + r
            same = (rows_of[:, r + 1 : r + 2] == target) & (number < limit)
            latest = jnp.maximum(latest, jnp.where(same, number + 1, 0))
        table_v[0:1, :] = listed
        table_v[1:2, :] = jnp.max(latest, axis=0, keepdims=True)
        table_store = pltpu.make_async_copy(table_v, table, table_sem)
        table_store.start()
        table_store.wait()

    send_in(0, 0)
    send_in(0, 1)
    make_table()

    def project(w_v):
        w_load = pltpu.make_async_copy(w_hbm, w_v, load_sem.at[len(loads)])
        w_load.start()
        send_picks(0, 0)
        relay_cotangent()
        send_picks(0, 1)
        send_in(1, 0)
        send_in(1, 1)
        w_load.wait()
        for copy in loads:
            copy.wait()
        wait_cotangent()
        depth = og_v.shape[2]
        half = depth // 2
        for pair in range(HEADS_HERE // 2):
            rows = pl.ds(pair * 2 * HEAD_DIM, 2 * HEAD_DIM)

            def add(t, result, rows=rows):
                part = pl.ds(pl.multiple_of(t % 2 * half, half), half)
                columns = pl.ds(pl.multiple_of(t * half, half), half)
                return result + dot_nt(og_v[t // 2, :, part], w_v[rows, columns])

            result = lax.fori_loop(
                0, 2 * ZDEV, add, jnp.zeros((BLOCK, 2 * HEAD_DIM), jnp.float32)
            )
            for k in range(2):
                g_v[pair * 2 + k] = result[:, k * HEAD_DIM : (k + 1) * HEAD_DIM].astype(jnp.bfloat16)

    pl.run_scoped(project, pltpu.VMEM(w_hbm.shape, jnp.bfloat16))
    wait_picks(0, 0)
    wait_picks(0, 1)

    def attend(p_s, dp_s):
        def one_head(head, carry):
            c = head // GROUP

            @pl.when(head == 1)
            def _():
                send_picks(1, 0)

            @pl.when(head == 3)
            def _():
                send_picks(1, 1)

            @pl.when(head == GROUP)
            def _():
                send_back(0, 0)
                send_back(0, 1)
                wait_picks(1, 0)
                wait_picks(1, 1)

            @pl.when(head == GROUP + 1)
            def _():
                send_home(0, 0)

            @pl.when(head == GROUP + 2)
            def _():
                send_home(0, 1)

            @pl.when(head % GROUP == 0)
            def _():
                acc[...] = jnp.zeros_like(acc)

            query = q_v[head]
            grad = g_v[head]

            def tiles(slot):
                key = kv[c, 0, slot].reshape(BLOCK, HEAD_DIM)
                value = kv[c, 1, slot].reshape(BLOCK, HEAD_DIM)
                return key, value

            def forward(slot, state):
                key, value = tiles(slot)
                scores = dot_nt(key, query)
                if state is None:
                    key_at = lax.broadcasted_iota(jnp.int32, (BLOCK, BLOCK), 0)
                    query_at = lax.broadcasted_iota(jnp.int32, (BLOCK, BLOCK), 1)
                    scores = jnp.where(key_at <= query_at, scores, -jnp.inf)
                    top = jnp.max(scores, axis=0, keepdims=True)
                else:
                    top = jnp.maximum(state[0], jnp.max(scores, axis=0, keepdims=True))
                shifted = jnp.exp2((scores - top) * EXP2_SCALE)
                grad_weights = dot_nt(value, grad)
                p_s[slot] = shifted
                dp_s[slot] = grad_weights
                stats[slot] = top
                norm = jnp.sum(shifted, axis=0, keepdims=True)
                row_dot = jnp.sum(shifted * grad_weights, axis=0, keepdims=True)
                if state is not None:
                    shrink = jnp.exp2((state[0] - top) * EXP2_SCALE)
                    norm = norm + state[1] * shrink
                    row_dot = row_dot + state[2] * shrink
                return top, norm, row_dot

            state = forward(0, None)
            top, norm, row_dot = lax.fori_loop(1, TOPK, forward, state)
            inverse = 1.0 / norm
            row_dot = row_dot * inverse

            def backward(slot, query_part):
                key, _ = tiles(slot)
                weights = p_s[slot] * (jnp.exp2((stats[slot] - top) * EXP2_SCALE) * inverse)
                weights_low = weights.astype(jnp.bfloat16)
                grad_low = (weights * (dp_s[slot] - row_dot)).astype(jnp.bfloat16)
                acc[1, slot] += dot_nn(weights_low, grad)
                acc[0, slot] += dot_nn(grad_low, query)
                return query_part + dot_tn(key, grad_low)

            query_part = jnp.zeros((HEAD_DIM, BLOCK), jnp.float32)
            for slot in range(TOPK):
                query_part = backward(slot, query_part)
            columns = pl.ds(pl.multiple_of(head * HEAD_DIM, HEAD_DIM), HEAD_DIM)
            dq_out[:, columns] = jnp.transpose(query_part * FACTOR).astype(jnp.bfloat16)
            return carry

        lax.fori_loop(0, HEADS_HERE, one_head, 0)

    pl.run_scoped(
        attend,
        pltpu.VMEM((TOPK, BLOCK, BLOCK), jnp.float32),
        pltpu.VMEM((TOPK, BLOCK, BLOCK), jnp.float32),
    )
    send_back(1, 0)
    send_back(1, 1)
    send_home(1, 0)
    send_home(1, 1)
    for c in range(KV_HERE):
        for a in range(2):
            finish(c, a)


def shards(queries, keys, values, out_grad, out_weight, selected):
    bf16, f32 = jnp.bfloat16, jnp.float32
    kv_cols = keys.shape[1]
    tiled = (RUN, SEQ, PIECE, kv_cols)
    tile = (PIECE, HEAD_DIM)
    dma = pltpu.SemaphoreType.DMA
    hbm = pl.BlockSpec(memory_space=pltpu.HBM)
    vmem = pl.BlockSpec(memory_space=pltpu.VMEM)
    query_grad, key_grad, value_grad = pl.pallas_call(
        kernel,
        out_shape=(
            pltpu.VMEM(queries.shape, bf16),
            pltpu.VMEM(tiled, bf16),
            pltpu.VMEM(tiled, bf16),
        ),
        in_specs=[hbm] * 6,
        out_specs=(vmem, vmem, vmem),
        scratch_shapes=[
            pltpu.VMEM(selected.shape[::-1], jnp.int32),
            pltpu.VMEM((2, TABLE), jnp.int32),
            pltpu.SMEM((2, TABLE), jnp.int32),
            pltpu.VMEM((HEADS_HERE, BLOCK, HEAD_DIM), bf16),
            pltpu.VMEM((HEADS_HERE, BLOCK, HEAD_DIM), bf16),
            pltpu.VMEM((ZDEV, *out_grad.shape), bf16),
            *[pltpu.VMEM((KBLOCKS, *tile), bf16)] * 2 * KV_HERE,
            pltpu.VMEM((KV_HERE, 2, SEQ, SLOTS, *tile), bf16),
            pltpu.VMEM((KV_HERE, 2, TOPK, SEQ, *tile), bf16),
            pltpu.VMEM((2, TOPK, BLOCK, HEAD_DIM), f32),
            pltpu.VMEM((KV_HERE, 2, TOPK, SEQ, *tile), bf16),
            pltpu.VMEM((KV_HERE, 2, SEQ, SLOTS, *tile), bf16),
            pltpu.VMEM((SEQ * SLOTS + 1, *tile), f32),
            pltpu.VMEM((KV_HERE, 2, KBLOCKS, *tile), bf16),
            pltpu.VMEM((TOPK, 1, BLOCK), f32),
            *[dma((KV_HERE, 2))] * 8,
            dma((4,)),
            dma((4,)),
            dma((4, KV_HERE, 2)),
            dma((HEADS_HERE + 6,)),
            dma,
        ],
        compiler_params=pltpu.CompilerParams(
            collective_id=0, has_side_effects=True, vmem_limit_bytes=56 << 20
        ),
    )(
        selected.T, queries, keys.reshape(tiled), values.reshape(tiled), out_grad, out_weight
    )
    return query_grad, key_grad.reshape(keys.shape), value_grad.reshape(values.shape)


def solution(mesh):
    in_specs = (
        P("seq", "head"),
        P("seq", "head"),
        P("seq", "head"),
        P("seq", "head"),
        P("head", None),
        P(),
    )
    out_specs = (P("seq", "head"), P("seq", "head"), P("seq", "head"))
    return jax.shard_map(shards, mesh=mesh, in_specs=in_specs, out_specs=out_specs, check_vma=False)
```

```python
import functools
import math

import jax
import jax.numpy as jnp
from jax import lax
from jax.experimental import pallas as pl
from jax.experimental.pallas import tpu as pltpu
from jax.sharding import PartitionSpec as P

HEAD_DIM = 128
BLOCK = 512
TOPK = 6
SEQ = 32
ZDEV = 4
RUN = 8
PIECE = BLOCK // SEQ
SLOTS = TOPK - 1
KBLOCKS = SEQ * RUN
TABLE = 512
HEADS_HERE = 8
KV_HERE = 2
GROUP = HEADS_HERE // KV_HERE
FACTOR = HEAD_DIM**-0.5
EXP2_SCALE = FACTOR * math.log2(math.e)
MESH = pl.DeviceIdType.MESH

OFFSETS = [
    (2, 2), (1, 2), (2, 1), (3, 2), (2, 3), (1, 1), (3, 3), (1, 3),
    (3, 1), (2, 0), (0, 2), (1, 0), (3, 0), (0, 1), (0, 3),
]
DX_CODE = sum(dx * 4**t for t, (dx, _) in enumerate(OFFSETS))
DY_CODE = sum(dy * 4**t for t, (_, dy) in enumerate(OFFSETS))


def each_peer(me, visit):
    x, y, core = me // 8, me // 2 % 4, me % 2

    def step(flip, codes):
        dx_code, dy_code = codes
        peer = (x + dx_code % 4) % 4 * 8 + (y + dy_code % 4) % 4 * 2 + (core + flip) % 2
        visit(peer)
        return dx_code // 4, dy_code // 4

    for flip in (0, 1):
        lax.fori_loop(
            0,
            len(OFFSETS),
            lambda t, codes, flip=flip: step(flip, codes),
            (DX_CODE + core * (DY_CODE - DX_CODE), DY_CODE + core * (DX_CODE - DY_CODE)),
        )
    visit(x * 8 + y * 2 + 1 - core)


def dot_nt(a, b):
    return lax.dot_general(a, b, (((1,), (1,)), ((), ())), preferred_element_type=jnp.float32)


def dot_nn(a, b):
    return jnp.dot(a, b, preferred_element_type=jnp.float32)


def dot_tn(a, b):
    return lax.dot_general(a, b, (((0,), (0,)), ((), ())), preferred_element_type=jnp.float32)


def head_cols(index):
    return pl.ds(index * HEAD_DIM, HEAD_DIM)


def kernel(
    selected, q_hbm, k_hbm, v_hbm, og_hbm, w_hbm,
    dq_out, dk_out, dv_out,
    selected_v, table_v, table, q_v, g_v, og_v, pool_0, pool_1, pool_2, pool_3, stage, kv, acc, piece, came,
    running, total, stats,
    in_send, in_recv, pick_send, pick_recv, back_send, back_recv, home_send, home_recv,
    og_send, og_recv, self_move, load_sem, table_sem,
):
    me = lax.axis_index("seq")
    z = lax.axis_index("head")
    pool = ((pool_0, pool_1), (pool_2, pool_3))

    def remote(src, dst, send_sem, recv_sem, peer, peer_z=None):
        pltpu.make_async_remote_copy(
            src_ref=src, dst_ref=dst, send_sem=send_sem, recv_sem=recv_sem,
            device_id=(peer, z if peer_z is None else peer_z), device_id_type=MESH,
        ).start()

    def wait_for(ref, sem):
        pltpu.make_async_copy(ref, ref, sem).wait()

    table_load = pltpu.make_async_copy(selected, selected_v, table_sem)
    table_load.start()
    loads = []

    def load(src, dst):
        copy = pltpu.make_async_copy(src, dst, load_sem.at[len(loads)])
        copy.start()
        loads.append(copy)

    load(og_hbm, og_v.at[z])
    for head in range(HEADS_HERE):
        load(q_hbm.at[:, head_cols(head)], q_v.at[head])
    for c in range(KV_HERE):
        for a, ref in enumerate((k_hbm, v_hbm)):
            load(ref.at[RUN - 1, :, :, head_cols(c)], kv.at[c, a, 0])

    barrier = pltpu.get_barrier_semaphore()

    def greet(t, carry):
        pl.semaphore_signal(
            barrier, inc=1, device_id=((me + t) % SEQ, z), device_id_type=MESH
        )
        return carry

    lax.fori_loop(1, SEQ, greet, 0)
    for t in range(1, ZDEV):
        pl.semaphore_signal(barrier, inc=1, device_id=(me, (z + t) % ZDEV), device_id_type=MESH)
    pl.semaphore_wait(barrier, SEQ - 1 + ZDEV - 1)

    above, below = (z + 1) % ZDEV, (z + ZDEV - 1) % ZDEV
    remote(og_hbm, og_v.at[z], og_send.at[0], og_recv.at[0], me, above)
    remote(og_hbm, og_v.at[z], og_send.at[1], og_recv.at[1], me, below)

    def relay_cotangent():
        half = og_v.shape[1] // 2
        for way, (source, target) in enumerate(((below, above), (above, below))):
            wait_for(og_v.at[source], og_recv.at[way])
            part = og_v.at[source, pl.ds(way * half, half)]
            remote(part, part, og_send.at[2 + way], og_recv.at[2 + way], me, target)

    def wait_cotangent():
        half = og_v.at[0, pl.ds(0, og_v.shape[1] // 2)]
        for way in range(2):
            wait_for(og_v.at[0], og_send.at[way])
            wait_for(half, og_send.at[2 + way])
            wait_for(half, og_recv.at[2 + way])

    def send_in(c, a):
        ref = (k_hbm, v_hbm)[a]
        mine = pool[c][a].at[pl.ds(me * RUN, RUN)]
        pltpu.make_async_copy(
            ref.at[:, me, :, head_cols(c)], mine, self_move.at[0, c, a]
        ).start()
        each_peer(
            me,
            lambda peer: remote(
                ref.at[:, peer, :, head_cols(c)], mine,
                in_send.at[c, a], in_recv.at[c, a], peer,
            ),
        )

    def send_picks(c, a):
        others = pool[c][a].at[pl.ds(0, (SEQ - 1) * RUN)]
        wait_for(others, in_recv.at[c, a])
        wait_for(others, in_send.at[c, a])
        wait_for(pool[c][a].at[pl.ds(0, RUN)], self_move.at[0, c, a])

        def choose(i, carry):
            for r in range(SLOTS):
                stage[c, a, i, r] = pool[c][a][table[0, i * SLOTS + r]]
            return carry

        lax.fori_loop(0, SEQ, choose, 0)
        mine = kv.at[c, a, pl.ds(1, SLOTS), me]
        pltpu.make_async_copy(stage.at[c, a, me], mine, self_move.at[1, c, a]).start()
        each_peer(
            me,
            lambda peer: remote(
                stage.at[c, a, peer], mine, pick_send.at[c, a], pick_recv.at[c, a], peer
            ),
        )

    def wait_picks(c, a):
        others = stage.at[c, a, pl.ds(0, SEQ - 1)]
        wait_for(others, pick_recv.at[c, a])
        wait_for(others, pick_send.at[c, a])
        wait_for(stage.at[c, a, 0], self_move.at[1, c, a])

    def send_back(c, a):
        for slot in range(TOPK):
            value = acc[a, slot]
            if a == 0:
                value = value * FACTOR
            piece[c, a, slot] = value.astype(jnp.bfloat16).reshape(SEQ, PIECE, HEAD_DIM)
        mine = came.at[c, a, me]
        pltpu.make_async_copy(
            piece.at[c, a, pl.ds(1, SLOTS), me], mine, self_move.at[2, c, a]
        ).start()
        each_peer(
            me,
            lambda peer: remote(
                piece.at[c, a, pl.ds(1, SLOTS), peer], mine,
                back_send.at[c, a], back_recv.at[c, a], peer,
            ),
        )

    def send_home(c, a):
        others = came.at[c, a, pl.ds(0, SEQ - 1)]
        wait_for(others, back_recv.at[c, a])
        wait_for(others, back_send.at[c, a])
        wait_for(came.at[c, a, 0], self_move.at[2, c, a])
        running[0] = jnp.zeros_like(running[0])

        def add(i, carry):
            for r in range(SLOTS):
                number = i * SLOTS + r
                running[number + 1] = (
                    came[c, a, i, r].astype(jnp.float32) + running[table[1, number]]
                )
            return carry

        lax.fori_loop(0, SEQ, add, 0)

        def gather(j, carry):
            for k in range(RUN):
                block = j * RUN + k
                total[c, a, block] = running[table[1, SEQ * SLOTS + block]].astype(jnp.bfloat16)
            return carry

        lax.fori_loop(0, SEQ, gather, 0)
        mine = (dk_out, dv_out)[a].at[:, me, :, head_cols(c)]
        pltpu.make_async_copy(
            total.at[c, a, pl.ds(me * RUN, RUN)], mine, self_move.at[3, c, a]
        ).start()
        each_peer(
            me,
            lambda peer: remote(
                total.at[c, a, pl.ds(peer * RUN, RUN)], mine,
                home_send.at[c, a], home_recv.at[c, a], peer,
            ),
        )

    def finish(c, a):
        others = total.at[c, a, pl.ds(0, (SEQ - 1) * RUN)]
        wait_for(others, home_recv.at[c, a])
        wait_for(others, home_send.at[c, a])
        wait_for(total.at[c, a, pl.ds(0, RUN)], self_move.at[3, c, a])
        ref, columns = (dk_out, dv_out)[a], head_cols(c)
        own = ref[RUN - 1, :, :, columns].astype(jnp.float32)
        own = own + piece[c, a, 0].astype(jnp.float32)
        ref[RUN - 1, :, :, columns] = own.astype(jnp.bfloat16)

    def make_table():
        table_load.wait()
        rows_of = jnp.transpose(selected_v[...])
        lane = lax.broadcasted_iota(jnp.int32, (SEQ, table_v.shape[1]), 1)
        row = lax.broadcasted_iota(jnp.int32, (SEQ, table_v.shape[1]), 0)
        count = SEQ * SLOTS
        listed = jnp.zeros_like(lane)
        for r in range(SLOTS):
            listed += jnp.where(lane == row * SLOTS + r, rows_of[:, r + 1 : r + 2], 0)
        listed = jnp.sum(listed, axis=0, keepdims=True)
        target = jnp.where(lane < count, listed, lane - count)
        limit = jnp.minimum(lane, count)
        latest = jnp.zeros_like(lane)
        for r in range(SLOTS):
            number = row * SLOTS + r
            same = (rows_of[:, r + 1 : r + 2] == target) & (number < limit)
            latest = jnp.maximum(latest, jnp.where(same, number + 1, 0))
        table_v[0:1, :] = listed
        table_v[1:2, :] = jnp.max(latest, axis=0, keepdims=True)
        table_store = pltpu.make_async_copy(table_v, table, table_sem)
        table_store.start()
        table_store.wait()

    send_in(0, 0)
    send_in(0, 1)
    make_table()

    def project(w_v, partial):
        w_load = pltpu.make_async_copy(w_hbm, w_v, load_sem.at[len(loads)])
        w_load.start()
        send_picks(0, 0)
        relay_cotangent()
        send_picks(0, 1)
        send_in(1, 0)
        send_in(1, 1)
        w_load.wait()
        for copy in loads:
            copy.wait()
        depth = og_v.shape[2]
        half = depth // 2

        def product(pair, shift, side):
            rows = pl.ds(pair * 2 * HEAD_DIM, 2 * HEAD_DIM)
            source = (z + shift) % ZDEV
            part = pl.ds(pl.multiple_of(side * half, half), half)
            columns = pl.ds(pl.multiple_of(source * depth + side * half, half), half)
            return dot_nt(og_v[source, :, part], w_v[rows, columns])

        for pair in range(HEADS_HERE // 2):
            partial[pair] = lax.fori_loop(
                0,
                2 * (ZDEV - 1),
                lambda t, result, pair=pair: result + product(pair, t // 2 + t // 4, t % 2),
                jnp.zeros((BLOCK, 2 * HEAD_DIM), jnp.float32),
            )
        wait_cotangent()
        for pair in range(HEADS_HERE // 2):
            result = partial[pair] + product(pair, 2, 0) + product(pair, 2, 1)
            for k in range(2):
                columns = slice(k * HEAD_DIM, (k + 1) * HEAD_DIM)
                g_v[pair * 2 + k] = result[:, columns].astype(jnp.bfloat16)

    pl.run_scoped(
        project,
        pltpu.VMEM(w_hbm.shape, jnp.bfloat16),
        pltpu.VMEM((HEADS_HERE // 2, BLOCK, 2 * HEAD_DIM), jnp.float32),
    )
    wait_picks(0, 0)
    wait_picks(0, 1)

    def attend(p_s, dp_s):
        def one_head(head, carry):
            c = head // GROUP

            @pl.when(head == 1)
            def _():
                send_picks(1, 0)

            @pl.when(head == 3)
            def _():
                send_picks(1, 1)

            @pl.when(head == GROUP)
            def _():
                send_back(0, 0)
                send_back(0, 1)
                wait_picks(1, 0)
                wait_picks(1, 1)

            @pl.when(head == GROUP + 1)
            def _():
                send_home(0, 0)

            @pl.when(head == GROUP + 2)
            def _():
                send_home(0, 1)

            @pl.when(head % GROUP == 0)
            def _():
                acc[...] = jnp.zeros_like(acc)

            query = q_v[head]
            grad = g_v[head]

            def tiles(slot):
                key = kv[c, 0, slot].reshape(BLOCK, HEAD_DIM)
                value = kv[c, 1, slot].reshape(BLOCK, HEAD_DIM)
                return key, value

            def forward(slot, state):
                key, value = tiles(slot)
                scores = dot_nt(key, query)
                if state is None:
                    key_at = lax.broadcasted_iota(jnp.int32, (BLOCK, BLOCK), 0)
                    query_at = lax.broadcasted_iota(jnp.int32, (BLOCK, BLOCK), 1)
                    scores = jnp.where(key_at <= query_at, scores, -jnp.inf)
                    top = jnp.max(scores, axis=0, keepdims=True)
                else:
                    top = jnp.maximum(state[0], jnp.max(scores, axis=0, keepdims=True))
                shifted = jnp.exp2((scores - top) * EXP2_SCALE)
                grad_weights = dot_nt(value, grad)
                p_s[slot] = shifted
                dp_s[slot] = grad_weights
                stats[slot] = top
                norm = jnp.sum(shifted, axis=0, keepdims=True)
                row_dot = jnp.sum(shifted * grad_weights, axis=0, keepdims=True)
                if state is not None:
                    shrink = jnp.exp2((state[0] - top) * EXP2_SCALE)
                    norm = norm + state[1] * shrink
                    row_dot = row_dot + state[2] * shrink
                return top, norm, row_dot

            state = forward(0, None)
            top, norm, row_dot = lax.fori_loop(1, TOPK, forward, state)
            inverse = 1.0 / norm
            row_dot = row_dot * inverse

            def backward(slot, query_part):
                key, _ = tiles(slot)
                weights = p_s[slot] * (jnp.exp2((stats[slot] - top) * EXP2_SCALE) * inverse)
                weights_low = weights.astype(jnp.bfloat16)
                grad_low = (weights * (dp_s[slot] - row_dot)).astype(jnp.bfloat16)
                acc[1, slot] += dot_nn(weights_low, grad)
                acc[0, slot] += dot_nn(grad_low, query)
                return query_part + dot_tn(key, grad_low)

            query_part = jnp.zeros((HEAD_DIM, BLOCK), jnp.float32)
            for slot in range(TOPK):
                query_part = backward(slot, query_part)
            columns = pl.ds(pl.multiple_of(head * HEAD_DIM, HEAD_DIM), HEAD_DIM)
            dq_out[:, columns] = jnp.transpose(query_part * FACTOR).astype(jnp.bfloat16)
            return carry

        lax.fori_loop(0, HEADS_HERE, one_head, 0)

    pl.run_scoped(
        attend,
        pltpu.VMEM((TOPK, BLOCK, BLOCK), jnp.float32),
        pltpu.VMEM((TOPK, BLOCK, BLOCK), jnp.float32),
    )
    send_back(1, 0)
    send_back(1, 1)
    send_home(1, 0)
    send_home(1, 1)
    for c in range(KV_HERE):
        for a in range(2):
            finish(c, a)


def shards(queries, keys, values, out_grad, out_weight, selected):
    bf16, f32 = jnp.bfloat16, jnp.float32
    kv_cols = keys.shape[1]
    tiled = (RUN, SEQ, PIECE, kv_cols)
    tile = (PIECE, HEAD_DIM)
    dma = pltpu.SemaphoreType.DMA
    hbm = pl.BlockSpec(memory_space=pltpu.HBM)
    vmem = pl.BlockSpec(memory_space=pltpu.VMEM)
    query_grad, key_grad, value_grad = pl.pallas_call(
        kernel,
        out_shape=(
            pltpu.VMEM(queries.shape, bf16),
            pltpu.VMEM(tiled, bf16),
            pltpu.VMEM(tiled, bf16),
        ),
        in_specs=[hbm] * 6,
        out_specs=(vmem, vmem, vmem),
        scratch_shapes=[
            pltpu.VMEM(selected.shape[::-1], jnp.int32),
            pltpu.VMEM((2, TABLE), jnp.int32),
            pltpu.SMEM((2, TABLE), jnp.int32),
            pltpu.VMEM((HEADS_HERE, BLOCK, HEAD_DIM), bf16),
            pltpu.VMEM((HEADS_HERE, BLOCK, HEAD_DIM), bf16),
            pltpu.VMEM((ZDEV, *out_grad.shape), bf16),
            *[pltpu.VMEM((KBLOCKS, *tile), bf16)] * 2 * KV_HERE,
            pltpu.VMEM((KV_HERE, 2, SEQ, SLOTS, *tile), bf16),
            pltpu.VMEM((KV_HERE, 2, TOPK, SEQ, *tile), bf16),
            pltpu.VMEM((2, TOPK, BLOCK, HEAD_DIM), f32),
            pltpu.VMEM((KV_HERE, 2, TOPK, SEQ, *tile), bf16),
            pltpu.VMEM((KV_HERE, 2, SEQ, SLOTS, *tile), bf16),
            pltpu.VMEM((SEQ * SLOTS + 1, *tile), f32),
            pltpu.VMEM((KV_HERE, 2, KBLOCKS, *tile), bf16),
            pltpu.VMEM((TOPK, 1, BLOCK), f32),
            *[dma((KV_HERE, 2))] * 8,
            dma((4,)),
            dma((4,)),
            dma((4, KV_HERE, 2)),
            dma((HEADS_HERE + 6,)),
            dma,
        ],
        compiler_params=pltpu.CompilerParams(
            collective_id=0, has_side_effects=True, vmem_limit_bytes=56 << 20
        ),
    )(
        selected.T, queries, keys.reshape(tiled), values.reshape(tiled), out_grad, out_weight
    )
    return query_grad, key_grad.reshape(keys.shape), value_grad.reshape(values.shape)


def solution(mesh):
    in_specs = (
        P("seq", "head"),
        P("seq", "head"),
        P("seq", "head"),
        P("seq", "head"),
        P("head", None),
        P(),
    )
    out_specs = (P("seq", "head"), P("seq", "head"), P("seq", "head"))
    return jax.shard_map(shards, mesh=mesh, in_specs=in_specs, out_specs=out_specs, check_vma=False)
```
